32 devices in a mesh: dp: 4 (over x, core), group: 8 (over z, y).
Axes of the slice: x: 2, y: 2, z: 4, core: 2. Of those that a mesh axis runs over, the one named last changes fastest.
Arguments:
- image_tiles: bfloat16 [4, 8, 8, 4, 4, 352], P('dp', 'group'), may hold values from -6 to 6
- cotangent: bfloat16 [4, 8, 8, 4, 4, 352], P('dp', 'group'), may hold values from -6 to 6
- image_rows: int32 [4, 8], P('dp', 'group'), may hold values from 1 to 2, as said below
- dw_kernel: float32 [7, 7, 352], replicated, may hold values from -0.875 to 0.875
- dw_bias: float32 [352], replicated, may hold values from -1 to 1
- layer_norm_gain: float32 [352], replicated, may hold values from 0.1 to 1.9
- layer_norm_bias: float32 [352], replicated, may hold values from -3 to 3
- weight_in: bfloat16 [352, 1408], replicated, may hold values from -0.3125 to 0.3125
- bias_in: float32 [1408], replicated, may hold values from -2.5 to 1
- grn_gamma: float32 [1408], replicated, may hold values from -1 to 1
- grn_beta: float32 [1408], replicated, may hold values from -3 to 3
- weight_out: bfloat16 [1408, 352], replicated, may hold values from -0.15625 to 0.15625
- bias_out: float32 [352], replicated, may hold values from -3 to 3
Outputs:
- outputs: bfloat16 [4, 8, 8, 4, 4, 352], P('dp', 'group')
- input_grads: bfloat16 [4, 8, 8, 4, 4, 352], P('dp', 'group')
- grad_shards: float32 [32, 31696], P(('dp', 'group'))
The draws below stay inside these ranges and needn't reach their ends.
Inputs may be any that keep to these rules, and one draw needn't show every extreme that they name: `image_rows`: some device's image has all 2 tile rows.
All inputs are finite; a program needn't handle non-finite values.
Results may differ from the reference program's by a relative error of at most 0.0051.
Values may be sent and summed in bfloat16 or wider, within the bound.
No kernel may reach another device: no remote copies, remote signals or barrier semaphores. Data moves between devices by JAX's collectives and lax.ppermute only.
A program may use at most 64 MiB of HBM per device.

```python
import math
import jax
import jax.numpy as jnp
from jax import lax

C = 352
HID = 1408
KS = 7
TH = 4
TW = 4
GC = 4
GR = 2
RMIN = 1
PTOT = 1014112
SHARD = 31696
N_DP = 4
N_GROUP = 8
DEVICES = 32


def draw_image_rows(key, part):
    first_key, second_key = jax.random.split(key)
    loads = jax.random.randint(first_key, (N_DP * N_GROUP,), RMIN, GR + 1)
    position = jax.random.randint(second_key, (), 0, N_DP * N_GROUP)
    loads = loads.at[position].set(GR)
    return loads.reshape(N_DP, N_GROUP).astype(jnp.int32)


def shard_levels(key, dims, cuts, least, high):
    def one(dim, shards_of):
        steps = jax.random.uniform(jax.random.fold_in(jax.random.fold_in(key, 6), dim), (shards_of,), jnp.float32, least / len(cuts), high / len(cuts))
        return jnp.repeat(jnp.exp(steps), dims[dim] // shards_of).reshape((-1,) + (1,) * (len(dims) - dim - 1))

    factor_of = one(*cuts[0])
    for cut in cuts[1:]:
        factor_of = factor_of * one(*cut)
    return factor_of


def scatter_about(own_key, extent, spread, limit, cuts=(), held_as=jnp.bfloat16):
    entries = jax.random.normal(own_key, extent, jnp.float32) * spread
    if len(cuts) > 0:
        entries = shard_levels(own_key, extent, cuts, -0.22, 0.18) * entries
    return jnp.clip(entries, min=-limit, max=limit).astype(held_as)


def setup_inputs(seed: int = 0) -> dict:
    key_list = jax.random.split(jax.random.key(seed), 14)
    return {
        "image_tiles": scatter_about(key_list[0], (N_DP, N_GROUP, N_GROUP, TH, TW, C), 1.0, 6.0, ((0, 4), (1, 8))),
        "cotangent": scatter_about(key_list[1], (N_DP, N_GROUP, N_GROUP, TH, TW, C), 1.0, 6.0, ((0, 4), (1, 8))),
        "image_rows": draw_image_rows(jax.random.fold_in(key_list[13], 71), 0),
        "dw_kernel": scatter_about(key_list[3], (KS, KS, C), (KS * KS) ** -0.5, 0.875, (), jnp.float32),
        "dw_bias": jnp.clip(jax.random.uniform(key_list[4], (C,), jnp.float32, -1.0, 1.0), -1.0, 1.0),
        "layer_norm_gain": jnp.clip(1.0 + 0.18 * jax.random.normal(key_list[5], (C,), jnp.float32), 0.1, 1.9),
        "layer_norm_bias": scatter_about(key_list[6], (C,), 0.5, 3.0, (), jnp.float32),
        "weight_in": scatter_about(key_list[7], (C, HID), C ** -0.5, 0.3125),
        "bias_in": jnp.clip(jax.random.uniform(key_list[8], (HID,), jnp.float32, -2.5, 1.0), -2.5, 1.0),
        "grn_gamma": jnp.clip(jax.random.uniform(key_list[9], (HID,), jnp.float32, -1.0, 1.0), -1.0, 1.0),
        "grn_beta": scatter_about(key_list[10], (HID,), 0.5, 3.0, (), jnp.float32),
        "weight_out": scatter_about(key_list[11], (HID, C), HID ** -0.5, 0.15625),
        "bias_out": scatter_about(key_list[12], (C,), 0.5, 3.0, (), jnp.float32),
    }


def image_step(inputs, upstream, valid, dw_kernel, dw_bias, layer_norm_gain, layer_norm_bias, weight_in, bias_in, grn_gamma, grn_beta, weight_out, bias_out):
    height, width, channel_count = inputs.shape
    hidden_dim = weight_in.shape[1]
    total_row_count = height * width
    cell_mask = jnp.broadcast_to(valid, (height, width, 1)).reshape(total_row_count, 1)
    float_in = inputs.astype(jnp.float32)
    padded_in = jnp.pad(float_in, ((3, 3), (3, 3), (0, 0)))
    conv_out = jnp.zeros_like(float_in) + dw_bias
    for row_off in range(7):
        for col_off in range(7):
            conv_out = conv_out + padded_in[row_off:row_off + height, col_off:col_off + width, :] * dw_kernel[row_off, col_off]
    mean_c = lax.optimization_barrier(jnp.mean(conv_out, axis=-1, keepdims=True))
    centered_values = conv_out - mean_c
    inverse_deviation = lax.rsqrt(lax.optimization_barrier(jnp.mean(centered_values * centered_values, axis=-1, keepdims=True)) + 1e-06)
    standardized_input = centered_values * inverse_deviation
    normalized_output = (standardized_input * layer_norm_gain + layer_norm_bias).astype(jnp.bfloat16).reshape(total_row_count, channel_count)
    pre_act = jnp.dot(normalized_output, weight_in, preferred_element_type=jnp.float32) + bias_in
    act_out = 0.5 * pre_act * (1.0 + lax.erf(pre_act * 0.7071067811865476))
    act_kept = act_out * cell_mask
    norm_val = jnp.sqrt(1.0 + lax.optimization_barrier(jnp.sum(act_kept * act_kept, axis=0, keepdims=True)))
    denom = lax.optimization_barrier(jnp.mean(norm_val, axis=-1, keepdims=True)) + 1e-06
    scale_val = norm_val / denom
    mixed = (grn_gamma * (act_out * scale_val) + grn_beta + act_out).astype(jnp.bfloat16)
    branch = jnp.dot(mixed, weight_out, preferred_element_type=jnp.float32) + bias_out
    whole = float_in.reshape(total_row_count, channel_count) + branch
    result = jnp.where(cell_mask > 0, whole, jnp.zeros_like(whole)).astype(jnp.bfloat16).reshape(inputs.shape)
    up_rows = upstream.reshape(total_row_count, channel_count)
    up_float = up_rows.astype(jnp.float32)
    g_bias_out = lax.optimization_barrier(jnp.sum(up_float, axis=0))
    g_weight_out = lax.dot_general(mixed, up_rows, (((0,), (0,)), ((), ())), preferred_element_type=jnp.float32)
    d_mixed = lax.dot_general(up_rows, weight_out, (((1,), (1,)), ((), ())), preferred_element_type=jnp.float32)
    g_gamma = lax.optimization_barrier(jnp.sum(d_mixed * act_out * scale_val, axis=0))
    g_beta = lax.optimization_barrier(jnp.sum(d_mixed, axis=0))
    d_scale = lax.optimization_barrier(jnp.sum(d_mixed * grn_gamma * act_out, axis=0, keepdims=True))
    d_norm = d_scale / denom - lax.optimization_barrier(jnp.sum(d_scale * norm_val, axis=-1, keepdims=True)) / (denom * denom) / hidden_dim
    d_act = d_mixed * (grn_gamma * scale_val + 1.0) + act_kept * d_norm / norm_val
    cdf_val = 0.5 * (1.0 + lax.erf(pre_act * 0.7071067811865476))
    pdf_val = jnp.exp(-0.5 * pre_act * pre_act) * 0.3989422804014327
    d_pre = d_act * (cdf_val + pre_act * pdf_val)
    g_bias_in = lax.optimization_barrier(jnp.sum(d_pre, axis=0))
    d_pre_b = d_pre.astype(jnp.bfloat16)
    g_weight_in = lax.dot_general(normalized_output, d_pre_b, (((0,), (0,)), ((), ())), preferred_element_type=jnp.float32)
    normalized_gradient = lax.dot_general(d_pre_b, weight_in, (((1,), (1,)), ((), ())), preferred_element_type=jnp.float32).reshape(inputs.shape)
    layer_norm_gain_gradient = lax.optimization_barrier(jnp.sum(normalized_gradient * standardized_input, axis=(0, 1)))
    g_ln_bias = lax.optimization_barrier(jnp.sum(normalized_gradient, axis=(0, 1)))
    upscaled_values = normalized_gradient * layer_norm_gain
    conv_output_gradient = inverse_deviation * (upscaled_values - lax.optimization_barrier(jnp.mean(upscaled_values, axis=-1, keepdims=True)) - standardized_input * lax.optimization_barrier(jnp.mean(upscaled_values * standardized_input, axis=-1, keepdims=True)))
    g_dw_bias = lax.optimization_barrier(jnp.sum(conv_output_gradient, axis=(0, 1)))
    padded_grad = jnp.pad(conv_output_gradient, ((3, 3), (3, 3), (0, 0)))
    back_float = up_float.reshape(inputs.shape)
    kernel_rows = []
    for row_off in range(7):
        for col_off in range(7):
            kernel_rows.append(lax.optimization_barrier(jnp.sum(padded_in[row_off:row_off + height, col_off:col_off + width, :] * conv_output_gradient, axis=(0, 1))))
            back_float = back_float + padded_grad[6 - row_off:6 - row_off + height, 6 - col_off:6 - col_off + width, :] * dw_kernel[row_off, col_off]
    back_float = jnp.where(valid > 0, back_float, jnp.zeros_like(back_float))
    g_kernel = jnp.stack(kernel_rows)
    grad_flat = jnp.concatenate([g_kernel.reshape(-1), g_dw_bias, layer_norm_gain_gradient, g_ln_bias, g_weight_in.reshape(-1), g_bias_in, g_gamma, g_beta, g_weight_out.reshape(-1), g_bias_out])
    return (result, back_float.astype(jnp.bfloat16), grad_flat)

def to_canvas(tiles, grid_rows, grid_cols):
    slot_count, tile_h, tile_w, channel_count = tiles.shape
    return tiles.reshape(grid_rows, grid_cols, tile_h, tile_w, channel_count).transpose(0, 2, 1, 3, 4).reshape(grid_rows * tile_h, grid_cols * tile_w, channel_count)

def to_tiles(canvas, grid_rows, grid_cols, tile_h, tile_w):
    channel_count = canvas.shape[-1]
    return canvas.reshape(grid_rows, tile_h, grid_cols, tile_w, channel_count).transpose(0, 2, 1, 3, 4).reshape(grid_rows * grid_cols, tile_h, tile_w, channel_count)

def reference(image_tiles, cotangent, image_rows, dw_kernel, dw_bias, layer_norm_gain, layer_norm_bias, weight_in, bias_in, grn_gamma, grn_beta, weight_out, bias_out):
    received = jnp.swapaxes(image_tiles, 1, 2).reshape(N_DP * N_GROUP, N_GROUP, TH, TW, C)
    upstream = cotangent.reshape(N_DP * N_GROUP, N_GROUP, TH, TW, C)
    row_counts = image_rows.reshape(N_DP * N_GROUP)
    params = (dw_kernel, dw_bias, layer_norm_gain, layer_norm_bias, weight_in, bias_in, grn_gamma, grn_beta, weight_out, bias_out)
    cell_rows = jnp.arange(GR * TH, dtype=jnp.int32) // TH

    def visit(carry, item):
        tiles, grads_in, rows_used = item
        valid = (cell_rows < rows_used).astype(jnp.float32).reshape(GR * TH, 1, 1)
        canvas = to_canvas(tiles, GR, GC)
        canvas = jnp.where(valid > 0, canvas, jnp.zeros_like(canvas))
        up_canvas = to_canvas(grads_in, GR, GC)
        up_canvas = jnp.where(valid > 0, up_canvas, jnp.zeros_like(up_canvas))
        result, back_grads, grad_flat = image_step(canvas, up_canvas, valid, *params)
        return (carry + grad_flat, (to_tiles(result, GR, GC, TH, TW), to_tiles(back_grads, GR, GC, TH, TW)))
    summed, (results, backs) = lax.scan(visit, jnp.zeros((PTOT,), jnp.float32), (received, upstream, row_counts))
    outputs = results.reshape(N_DP, N_GROUP, N_GROUP, TH, TW, C)
    input_grads = jnp.swapaxes(backs.reshape(N_DP, N_GROUP, N_GROUP, TH, TW, C), 1, 2)
    padded = jnp.pad(summed, (0, DEVICES * SHARD - PTOT))
    factor = 1.0 / math.sqrt(N_DP * N_GROUP * N_GROUP * TH * TW)
    return (outputs, input_grads, (padded * factor).reshape(DEVICES, SHARD))
```

```python
import math
import functools

import jax
import jax.numpy as jnp
from jax import lax
from jax.experimental import pallas as pl
from jax.experimental.pallas import tpu as pltpu
from jax.sharding import PartitionSpec as P

GC = 4
LANES = 128
F32 = jnp.float32
BF16 = jnp.bfloat16


def partner(digit, step, count):
    if count & (count - 1) == 0:
        return digit ^ step, digit ^ step
    return (digit + step) % count, (digit + count - step) % count


class Plan:
    def __init__(self, data_count, group_count, total_len):
        self.nd, self.ng = data_count, group_count
        self.devices = data_count * group_count
        self.shard = (total_len + 8 * self.devices - 1) // (8 * self.devices) * 8
        self.rows = -(-(self.shard + LANES - 1) // LANES)
        self.rows = -(-self.rows // 16) * 16
        self.core = math.gcd(data_count, 2)
        self.dhi = data_count // self.core
        self.glo = math.gcd(group_count, 4)
        self.ghi = group_count // self.glo
        self.blocks = self.dhi * group_count
        self.cube = self.dhi * self.glo
        last = ((self.devices - 1) * self.shard) // LANES + self.rows
        self.flat_rows = -(-max(last, -(-total_len // LANES)) // 8) * 8

    def digits(self, d, g):
        return d // self.core, d % self.core, g // self.glo, g % self.glo

    def device(self, dhi, dlo, ghi, glo):
        return (dhi * self.core + dlo) * self.ng + ghi * self.glo + glo

    def pairs(self, core_step=0, cube_step=0, high_step=0):
        out = []
        for d in range(self.nd):
            for g in range(self.ng):
                dhi, dlo, ghi, glo = self.digits(d, g)
                to = self.device(
                    partner(dhi, cube_step // self.glo, self.dhi)[0],
                    partner(dlo, core_step, self.core)[0],
                    partner(ghi, high_step, self.ghi)[0],
                    partner(glo, cube_step % self.glo, self.glo)[0],
                )
                out.append((d * self.ng + g, to))
        return out


def pick_kernel(group_count, pos_ref, tiles_ref, *out_refs):
    g = pos_ref[1]
    for step in range(1, group_count):
        out_refs[step - 1][...] = tiles_ref[partner(g, step, group_count)[0]]


def store_wide(flat_ref, base, src_ref, rows, width):
    unit = LANES // math.gcd(width, LANES)
    groups = rows // unit
    per_group = unit * width // LANES
    lane = lax.broadcasted_iota(jnp.int32, (1, LANES), 1)
    step = 88
    for first in range(0, groups, step):
        count = min(step, groups - first)
        for block in range(per_group):
            begin, end = block * LANES, (block + 1) * LANES
            value = None
            for t in range(unit):
                lo, hi = max(begin, t * width), min(end, (t + 1) * width)
                if lo >= hi:
                    continue
                shift = (t * width) % LANES
                at = lo
                while at < hi:
                    piece = (at - t * width) // LANES
                    stop = min(hi, t * width + (piece + 1) * LANES)
                    part = src_ref[piece, pl.ds(t + unit * first, count, stride=unit), :]
                    if shift:
                        part = pltpu.roll(part, shift, 1)
                    if value is None:
                        value = part
                    else:
                        value = jnp.where(lane >= at - begin, part, value)
                    at = stop
            flat_ref[pl.ds(base + block + per_group * first, count, stride=per_group), :] = value


def image_kernel(
    plan,
    pos_ref,
    tiles_ref,
    *refs,
):
    group_count = plan.ng
    recv_refs = refs[: group_count - 1]
    (
        cot_ref, dwk_ref, dwb_ref, lng_ref, lnb_ref, win_ref, bin_ref, gam_ref, bet_ref,
        wout_ref, bout_ref,
    ) = refs[group_count - 1 : group_count + 10]
    outs = refs[group_count + 10 :]
    out_ref, own_ref = outs[:2]
    back_refs = outs[2 : group_count + 1]
    keep_ref, send_ref = outs[group_count + 1 : group_count + 3]
    (
        stage, pad, upc, conv, xhat, rstd_s, norm_b, act_s, gp_s, dmix_s, mixed_s, dpre_s,
        vecs, wide, small, gpad, backs, flat,
    ) = outs[group_count + 3 :]
    d, g, used = pos_ref[0], pos_ref[1], pos_ref[2]
    _, tile_h, tile_w, chans = tiles_ref.shape
    hid = win_ref.shape[1]
    grid_rows = group_count // GC
    height, width = grid_rows * tile_h, GC * tile_w
    cells = height * width
    edge = 8
    lanes_of = [(lo, min(lo + LANES, chans)) for lo in range(0, chans, LANES)]
    chunks = hid // LANES

    def put(at, line):
        for n, (lo, hi) in enumerate(lanes_of):
            small[n, at : at + 1, 0 : hi - lo] = line[:, lo:hi]

    stage[g] = tiles_ref[g].astype(F32)
    for step in range(1, group_count):
        stage[partner(g, step, group_count)[1]] = recv_refs[step - 1][...].astype(F32)
    pad[...] = jnp.zeros_like(pad)
    gpad[...] = jnp.zeros_like(gpad)
    for i in range(group_count):
        tr, tc = i // GC, i % GC
        ok = tr < used
        tile = jnp.where(ok, stage[i], 0.0)
        up = jnp.where(ok, cot_ref[i].astype(F32), 0.0)
        pad[3 + tr * tile_h : 3 + (tr + 1) * tile_h, edge + tc * tile_w : edge + (tc + 1) * tile_w, :] = tile
        upc[tr * tile_h : (tr + 1) * tile_h, tc * tile_w : (tc + 1) * tile_w, :] = up

    block_rows = 8
    for r0 in range(0, height, block_rows):
        for lo, hi in lanes_of:
            acc = jnp.broadcast_to(dwb_ref[:, lo:hi].reshape(1, 1, hi - lo), (block_rows, width, hi - lo))
            for b in range(7):
                part = pad[r0 : r0 + block_rows + 6, edge - 3 + b : edge - 3 + b + width, lo:hi]
                for a in range(7):
                    acc = acc + part[a : a + block_rows] * dwk_ref[a, b : b + 1, lo:hi].reshape(1, 1, hi - lo)
            conv[r0 * width : (r0 + block_rows) * width, lo:hi] = acc.reshape(block_rows * width, hi - lo)

    value = conv[...]
    mean = jnp.mean(value, axis=-1, keepdims=True)
    centered = value - mean
    rstd = lax.rsqrt(jnp.mean(centered * centered, axis=-1, keepdims=True) + 1e-06)
    hat = centered * rstd
    xhat[...] = hat
    rstd_s[...] = jnp.broadcast_to(rstd, rstd_s.shape)
    norm_b[...] = (hat * lng_ref[...] + lnb_ref[...]).astype(BF16)

    row = lax.broadcasted_iota(jnp.int32, (cells, 1), 0)
    mask = (row < used * (tile_h * width)).astype(F32)
    up_f = upc[...].reshape(cells, chans)
    up_b = up_f.astype(BF16)
    normed = norm_b[...]

    total_norm = jnp.zeros((1, 1), F32)
    for h in range(chunks):
        cols = slice(h * LANES, (h + 1) * LANES)
        pre = jnp.dot(normed, win_ref[:, cols], preferred_element_type=F32) + bin_ref[:, cols]
        cdf = 0.5 * (1.0 + lax.erf(pre * 0.7071067811865476))
        act = pre * cdf
        pdf = jnp.exp(-0.5 * pre * pre) * 0.3989422804014327
        act_s[:, cols] = act
        gp_s[:, cols] = cdf + pre * pdf
        kept = act * mask
        norm = jnp.sqrt(1.0 + jnp.sum(kept * kept, axis=0, keepdims=True))
        vecs[0:1, cols] = norm
        total_norm = total_norm + jnp.sum(norm, axis=-1, keepdims=True)
        dmix_s[:, cols] = lax.dot_general(
            up_b, wout_ref[cols, :], (((1,), (1,)), ((), ())), preferred_element_type=F32
        )
    den = total_norm / hid + 1e-06

    total_dn = jnp.zeros((1, 1), F32)
    for h in range(chunks):
        cols = slice(h * LANES, (h + 1) * LANES)
        act, dmix = act_s[:, cols], dmix_s[:, cols]
        norm = vecs[0:1, cols]
        scale = norm / den
        gamma = gam_ref[:, cols]
        mixed = (gamma * (act * scale) + bet_ref[:, cols] + act).astype(BF16)
        mixed_s[:, cols] = mixed
        grad = lax.dot_general(
            mixed, up_b, (((0,), (0,)), ((), ())), preferred_element_type=F32
        )
        for n, (lo, hi) in enumerate(lanes_of):
            wide[n, h * LANES : (h + 1) * LANES, 0 : hi - lo] = grad[:, lo:hi]
        along = jnp.sum(dmix * act, axis=0, keepdims=True)
        vecs[2:3, cols] = along * scale
        vecs[3:4, cols] = jnp.sum(dmix, axis=0, keepdims=True)
        d_scale = along * gamma
        vecs[4:5, cols] = d_scale
        total_dn = total_dn + jnp.sum(d_scale * norm, axis=-1, keepdims=True)
    pull = total_dn / (den * den) / hid

    head = (7 * 7 + 3) * chans // LANES
    for h in range(chunks):
        cols = slice(h * LANES, (h + 1) * LANES)
        act, dmix = act_s[:, cols], dmix_s[:, cols]
        norm = vecs[0:1, cols]
        scale = norm / den
        d_norm = vecs[4:5, cols] / den - pull
        d_act = dmix * (gam_ref[:, cols] * scale + 1.0) + act * mask * (d_norm / norm)
        d_pre = d_act * gp_s[:, cols]
        vecs[1:2, cols] = jnp.sum(d_pre, axis=0, keepdims=True)
        d_pre_b = d_pre.astype(BF16)
        dpre_s[:, cols] = d_pre_b
        flat[pl.ds(head + h, chans, stride=chunks), :] = lax.dot_general(
            normed, d_pre_b, (((0,), (0,)), ((), ())), preferred_element_type=F32
        )

    branch = jnp.dot(mixed_s[...], wout_ref[...], preferred_element_type=F32) + bout_ref[...]
    inner = pad[3 : 3 + height, edge : edge + width, :].reshape(cells, chans)
    conv[...] = jnp.where(mask > 0, inner + branch, 0.0)
    for i in range(group_count):
        tr, tc = i // GC, i % GC
        for a in range(tile_h):
            first = (tr * tile_h + a) * width + tc * tile_w
            out_ref[i, a] = conv[first : first + tile_w, :].astype(BF16)

    d_normed = lax.dot_general(
        dpre_s[...], win_ref[...], (((1,), (1,)), ((), ())), preferred_element_type=F32
    )
    hat = xhat[...]
    put(50, jnp.sum(d_normed * hat, axis=0, keepdims=True))
    put(51, jnp.sum(d_normed, axis=0, keepdims=True))
    e = d_normed * lng_ref[...]
    d_conv = rstd_s[:, 0:1] * (
        e
        - jnp.mean(e, axis=-1, keepdims=True)
        - hat * jnp.mean(e * hat, axis=-1, keepdims=True)
    )
    put(49, jnp.sum(d_conv, axis=0, keepdims=True))
    gpad[3 : 3 + height, edge : edge + width, :] = d_conv.reshape(height, width, chans)

    for n, (lo, hi) in enumerate(lanes_of):
        for b in range(7):
            sums = [None] * 7
            for r0 in range(0, height, block_rows):
                part = pad[r0 : r0 + block_rows + 6, edge - 3 + b : edge - 3 + b + width, lo:hi]
                grad = gpad[3 + r0 : 3 + r0 + block_rows, edge : edge + width, lo:hi]
                for a in range(7):
                    s = jnp.sum(part[a : a + block_rows] * grad, axis=0)
                    sums[a] = s if sums[a] is None else sums[a] + s
            for a in range(7):
                small[n, a * 7 + b : a * 7 + b + 1, 0 : hi - lo] = jnp.sum(sums[a], axis=0, keepdims=True)
        for r0 in range(0, height, block_rows):
            acc = upc[r0 : r0 + block_rows, :, lo:hi]
            for b in range(7):
                part = gpad[r0 : r0 + block_rows + 6, edge + 3 - b : edge + 3 - b + width, lo:hi]
                for a in range(7):
                    acc = acc + part[6 - a : 6 - a + block_rows] * dwk_ref[a, b : b + 1, lo:hi].reshape(1, 1, hi - lo)
            xhat[r0 * width : (r0 + block_rows) * width, lo:hi] = acc.reshape(block_rows * width, hi - lo)
    xhat[...] = jnp.where(mask > 0, xhat[...], 0.0)
    for i in range(group_count):
        tr, tc = i // GC, i % GC
        for a in range(tile_h):
            first = (tr * tile_h + a) * width + tc * tile_w
            backs[i, a] = xhat[first : first + tile_w, :]
    own_ref[...] = backs[g].astype(BF16)
    for step in range(1, group_count):
        back_refs[step - 1][...] = backs[partner(g, step, group_count)[0]].astype(BF16)

    store_wide(flat, 0, small, 7 * 7 + 3, chans)
    mid = head + chans * chunks
    for k in range(3):
        for h in range(chunks):
            flat[mid + k * chunks + h : mid + k * chunks + h + 1, :] = vecs[
                1 + k : 2 + k, h * LANES : (h + 1) * LANES
            ]
    late = mid + 3 * chunks
    store_wide(flat, late, wide, hid, chans)
    tail = late + chans * chunks
    flat[tail : plan.flat_rows, :] = jnp.zeros((plan.flat_rows - tail, LANES), F32)
    g_bias_out = jnp.sum(up_f, axis=0, keepdims=True)
    for n, (lo, hi) in enumerate(lanes_of):
        flat[tail + n : tail + n + 1, 0 : hi - lo] = g_bias_out[:, lo:hi]

    dlo = d % plan.core

    def cut(j, carry):
        dhi, rest = j // plan.ng, j % plan.ng
        mine = (dhi * plan.core + dlo) * plan.ng + rest
        keep_ref[j] = flat[pl.ds((mine * plan.shard) // LANES, plan.rows), :]
        if plan.core > 1:
            other = (dhi * plan.core + (1 - dlo)) * plan.ng + rest
            send_ref[j] = flat[pl.ds((other * plan.shard) // LANES, plan.rows), :].astype(BF16)
        return carry

    lax.fori_loop(0, plan.blocks, cut, 0)


def cube_kernel(plan, pos_ref, keep_ref, recv_ref, own_ref, *send_refs):
    dhi, _, _, glo = plan.digits(pos_ref[0], pos_ref[1])
    for m in range(plan.cube):
        to_d = partner(dhi, m // plan.glo, plan.dhi)[0]
        to_g = partner(glo, m % plan.glo, plan.glo)[0]
        for q in range(plan.ghi):
            j = to_d * plan.ng + q * plan.glo + to_g
            value = keep_ref[j]
            if plan.core > 1:
                value = value + recv_ref[j].astype(F32)
            if m == 0:
                own_ref[q] = value
            else:
                send_refs[m - 1][q] = value.astype(BF16)


def high_kernel(plan, pos_ref, keep_ref, *refs):
    recv_refs = refs[: plan.cube - 1]
    own_ref = refs[plan.cube - 1]
    send_refs = refs[plan.cube :]
    ghi = pos_ref[1] // plan.glo
    for r in range(plan.ghi):
        q = partner(ghi, r, plan.ghi)[0]
        value = keep_ref[q]
        for ref in recv_refs:
            value = value + ref[q].astype(F32)
        if r == 0:
            own_ref[...] = value
        else:
            send_refs[r - 1][...] = value.astype(BF16)


def last_kernel(plan, factor, pos_ref, keep_ref, *refs):
    high = plan.ghi - 1
    recv_refs = refs[:high]
    own_ref = refs[high]
    tile_refs = refs[high + 1 : high + plan.ng]
    out_ref, grads_ref = refs[high + plan.ng : high + plan.ng + 2]
    total = refs[-1]
    d, g = pos_ref[0], pos_ref[1]
    value = keep_ref[...]
    for ref in recv_refs:
        value = value + ref[...].astype(F32)
    shift = ((d * plan.ng + g) * plan.shard) % LANES
    lane = lax.broadcasted_iota(jnp.int32, (1, LANES), 1)
    total[0 : plan.rows, :] = pltpu.roll(value * factor, LANES - shift, 1)
    count = out_ref.shape[0]
    out_ref[...] = jnp.where(
        lane < LANES - shift, total[0:count, :], total[1 : count + 1, :]
    )
    grads_ref[g] = own_ref[...]
    for step in range(1, plan.ng):
        grads_ref[partner(g, step, plan.ng)[1]] = tile_refs[step - 1][...]


VM = pl.BlockSpec(memory_space=pltpu.VMEM)
SM = pl.BlockSpec(memory_space=pltpu.SMEM)


def call(kernel, inputs, out_shapes, scratch=(), name=None):
    return pl.pallas_call(
        kernel,
        in_specs=[SM] + [VM] * (len(inputs) - 1),
        out_specs=[VM] * len(out_shapes),
        out_shape=out_shapes,
        scratch_shapes=list(scratch),
        name=name,
    )(*inputs)


def per_device(
    image_tiles, cotangent, image_rows, dw_kernel, dw_bias, layer_norm_gain, layer_norm_bias,
    weight_in, bias_in, grn_gamma, grn_beta, weight_out, bias_out,
):
    axes = ("dp", "group")
    nd, ng = lax.axis_size("dp"), lax.axis_size("group")
    tiles = image_tiles[0, 0]
    _, tile_h, tile_w, chans = tiles.shape
    hid = weight_in.shape[1]
    total_len = 49 * chans + 3 * chans + 2 * chans * hid + 3 * hid + chans
    plan = Plan(nd, ng, total_len)
    height, width = (ng // GC) * tile_h, GC * tile_w
    cells = height * width
    pos = jnp.stack(
        [lax.axis_index("dp"), lax.axis_index("group"), image_rows[0, 0]]
    ).astype(jnp.int32)

    tile_shape = jax.ShapeDtypeStruct((tile_h, tile_w, chans), BF16)
    group_pairs = [
        [
            (i * ng + j, i * ng + partner(j, step, ng)[0])
            for i in range(nd)
            for j in range(ng)
        ]
        for step in range(1, ng)
    ]
    picked = call(
        functools.partial(pick_kernel, ng), (pos, tiles), [tile_shape] * (ng - 1), name="pick"
    )
    arrived = [lax.ppermute(x, axes, pairs) for x, pairs in zip(picked, group_pairs)]

    row = lambda v: v.reshape(1, -1)
    block = (plan.rows, LANES)
    wide = -(-chans // LANES)
    results = call(
        functools.partial(image_kernel, plan),
        (
            pos, tiles, *arrived, cotangent[0, 0], dw_kernel, row(dw_bias),
            row(layer_norm_gain), row(layer_norm_bias), weight_in, row(bias_in),
            row(grn_gamma), row(grn_beta), weight_out, row(bias_out),
        ),
        [jax.ShapeDtypeStruct(tiles.shape, BF16)]
        + [tile_shape] * ng
        + [
            jax.ShapeDtypeStruct((plan.blocks, *block), F32),
            jax.ShapeDtypeStruct((plan.blocks, *block), BF16),
        ],
        [
            pltpu.VMEM((ng, tile_h, tile_w, chans), F32),
            pltpu.VMEM((height + 6, width + 16, chans), F32),
            pltpu.VMEM((height, width, chans), F32),
            pltpu.VMEM((cells, chans), F32),
            pltpu.VMEM((cells, chans), F32),
            pltpu.VMEM((cells, LANES), F32),
            pltpu.VMEM((cells, chans), BF16),
            pltpu.VMEM((cells, hid), F32),
            pltpu.VMEM((cells, hid), F32),
            pltpu.VMEM((cells, hid), F32),
            pltpu.VMEM((cells, hid), BF16),
            pltpu.VMEM((cells, hid), BF16),
            pltpu.VMEM((8, hid), F32),
            pltpu.VMEM((wide, hid, LANES), F32),
            pltpu.VMEM((wide, 56, LANES), F32),
            pltpu.VMEM((height + 6, width + 16, chans), F32),
            pltpu.VMEM((ng, tile_h, tile_w, chans), F32),
            pltpu.VMEM((plan.flat_rows, LANES), F32),
        ],
        name="image",
    )
    outputs, own_back = results[:2]
    backs = results[2 : ng + 1]
    keep, send = results[ng + 1 :]

    recv = lax.ppermute(send, axes, plan.pairs(core_step=1)) if plan.core > 1 else send
    stack = (plan.ghi, *block)
    own, *sends = call(
        functools.partial(cube_kernel, plan),
        (pos, keep, recv),
        [jax.ShapeDtypeStruct(stack, F32)]
        + [jax.ShapeDtypeStruct(stack, BF16)] * (plan.cube - 1),
        name="cube",
    )
    recvs = [
        lax.ppermute(x, axes, plan.pairs(cube_step=m + 1)) for m, x in enumerate(sends)
    ]
    returned = [lax.ppermute(x, axes, pairs) for x, pairs in zip(backs, group_pairs)]
    own, *sends = call(
        functools.partial(high_kernel, plan),
        (pos, own, *recvs),
        [jax.ShapeDtypeStruct(block, F32)]
        + [jax.ShapeDtypeStruct(block, BF16)] * (plan.ghi - 1),
        name="high",
    )
    recvs = [
        lax.ppermute(x, axes, plan.pairs(high_step=r + 1)) for r, x in enumerate(sends)
    ]
    factor = 1.0 / math.sqrt(nd * ng * ng * tile_h * tile_w)
    out_rows = -(-plan.shard // LANES)
    shard, grads = call(
        functools.partial(last_kernel, plan, factor),
        (pos, own, *recvs, own_back, *returned),
        [
            jax.ShapeDtypeStruct((out_rows, LANES), F32),
            jax.ShapeDtypeStruct(tiles.shape, BF16),
        ],
        [pltpu.VMEM((plan.rows + 8, LANES), F32)],
        name="last",
    )
    shard = shard.reshape(1, -1)[:, : plan.shard]
    return (outputs[None, None], grads[None, None], shard)


def solution(mesh):
    tiled = P("dp", "group", None, None, None, None)
    return jax.shard_map(
        per_device,
        mesh=mesh,
        in_specs=(tiled, tiled, P("dp", "group")) + (P(),) * 10,
        out_specs=(tiled, tiled, P(("dp", "group"), None)),
        check_vma=False,
    )
```

```python
import math
import functools

import jax
import jax.numpy as jnp
from jax import lax
from jax.experimental import pallas as pl
from jax.experimental.pallas import tpu as pltpu
from jax.sharding import PartitionSpec as P

GC = 4
PARAMS = 11
LANES = 128
F32 = jnp.float32
BF16 = jnp.bfloat16


def partner(digit, step, count):
    if count & (count - 1) == 0:
        return digit ^ step, digit ^ step
    return (digit + step) % count, (digit + count - step) % count


class Plan:
    def __init__(self, data_count, group_count, total_len):
        self.nd, self.ng = data_count, group_count
        self.devices = data_count * group_count
        self.shard = (total_len + 8 * self.devices - 1) // (8 * self.devices) * 8
        self.rows = -(-(self.shard + LANES - 1) // LANES)
        self.rows = -(-self.rows // 16) * 16
        self.core = math.gcd(data_count, 2)
        self.dhi = data_count // self.core
        self.glo = math.gcd(group_count, 4)
        self.ghi = group_count // self.glo
        self.blocks = self.dhi * group_count
        self.cube = self.dhi * self.glo
        last = ((self.devices - 1) * self.shard) // LANES + self.rows
        self.flat_rows = -(-max(last, -(-total_len // LANES)) // 8) * 8

    def digits(self, d, g):
        return d // self.core, d % self.core, g // self.glo, g % self.glo

    def device(self, dhi, dlo, ghi, glo):
        return (dhi * self.core + dlo) * self.ng + ghi * self.glo + glo

    def order(self):
        def far(m):
            high, low = m // self.glo, m % self.glo
            return ((high > 0) + bin(low).count("1"), high == 0, m)

        return sorted(range(1, self.cube), key=far)

    def pairs(self, core_step=0, cube_step=0, high_step=0):
        out = []
        for d in range(self.nd):
            for g in range(self.ng):
                dhi, dlo, ghi, glo = self.digits(d, g)
                to = self.device(
                    partner(dhi, cube_step // self.glo, self.dhi)[0],
                    partner(dlo, core_step, self.core)[0],
                    partner(ghi, high_step, self.ghi)[0],
                    partner(glo, cube_step % self.glo, self.glo)[0],
                )
                out.append((d * self.ng + g, to))
        return out


def pick_kernel(plan, tiles_ref, *refs):
    out_refs, sems = refs[:-1], refs[-1]
    glo = lax.axis_index("group") % plan.glo
    copies = []
    for n, ref in enumerate(out_refs):
        to = partner(glo, n, plan.glo)[0]
        for q in range(plan.ghi):
            copies.append(
                pltpu.make_async_copy(
                    tiles_ref.at[q * plan.glo + to], ref.at[q], sems.at[n * plan.ghi + q]
                )
            )
    for copy in copies:
        copy.start()
    for copy in copies:
        copy.wait()


def turn_kernel(plan, *refs):
    in_refs, out_refs = refs[: plan.glo], refs[plan.glo :]
    ghi = lax.axis_index("group") // plan.glo
    for r, ref in enumerate(out_refs):
        q = partner(ghi, r, plan.ghi)[0]
        for n in range(plan.glo):
            ref[n] = in_refs[n][q]


def store_wide(flat_ref, base, src_ref, rows, width):
    unit = LANES // math.gcd(width, LANES)
    groups = rows // unit
    per_group = unit * width // LANES
    lane = lax.broadcasted_iota(jnp.int32, (1, LANES), 1)
    step = 88
    for first in range(0, groups, step):
        count = min(step, groups - first)
        for block in range(per_group):
            begin, end = block * LANES, (block + 1) * LANES
            value = None
            for t in range(unit):
                lo, hi = max(begin, t * width), min(end, (t + 1) * width)
                if lo >= hi:
                    continue
                shift = (t * width) % LANES
                at = lo
                while at < hi:
                    piece = (at - t * width) // LANES
                    stop = min(hi, t * width + (piece + 1) * LANES)
                    part = src_ref[piece, pl.ds(t + unit * first, count, stride=unit), :]
                    if shift:
                        part = pltpu.roll(part, shift, 1)
                    if value is None:
                        value = part
                    else:
                        value = jnp.where(lane >= at - begin, part, value)
                    at = stop
            flat_ref[pl.ds(base + block + per_group * first, count, stride=per_group), :] = value


def image_kernel(
    plan,
    rows_ref,
    *refs,
):
    group_count = plan.ng
    recv_refs, refs = refs[: plan.ghi], refs[plan.ghi :]
    params, refs = refs[:PARAMS], refs[PARAMS:]
    out_ref, back_ref, keep_ref, send_ref = refs[:4]
    held, refs = refs[4 : 4 + PARAMS], refs[4 + PARAMS :]
    (
        sems, stage, pad, upc, conv, xhat, rstd_s, norm_b, act_s, gp_s, dmix_s, mixed_s, dpre_s,
        vecs, wide, small, gpad, backs, flat,
    ) = refs
    copies = [
        pltpu.make_async_copy(source, target, sems.at[n])
        for n, (source, target) in enumerate(zip(params, held))
    ]
    for copy in copies:
        copy.start()
    (
        dwk_ref, dwb_ref, cot_ref, lng_ref, lnb_ref, win_ref, bin_ref, wout_ref, gam_ref,
        bet_ref, bout_ref,
    ) = held
    d, g, used = lax.axis_index("dp"), lax.axis_index("group"), rows_ref[0, 0]
    _, _, ghi, glo = plan.digits(d, g)
    _, tile_h, tile_w, chans = recv_refs[0].shape
    hid = win_ref.shape[1]
    grid_rows = group_count // GC
    height, width = grid_rows * tile_h, GC * tile_w
    cells = height * width
    edge = 8
    lanes_of = [(lo, min(lo + LANES, chans)) for lo in range(0, chans, LANES)]
    chunks = hid // LANES

    def line(ref, lo=0, hi=None):
        hi = ref.shape[0] if hi is None else hi
        return ref[lo:hi].reshape(1, hi - lo)

    def put(at, sums):
        for n, (lo, hi) in enumerate(lanes_of):
            small[n, at : at + 1, 0 : hi - lo] = sums[:, lo:hi]

    for r, ref in enumerate(recv_refs):
        for n in range(plan.glo):
            source = partner(ghi, r, plan.ghi)[1] * plan.glo + partner(glo, n, plan.glo)[1]
            stage[source] = ref[n].astype(F32)
    pad[...] = jnp.zeros_like(pad)
    gpad[...] = jnp.zeros_like(gpad)
    for i in range(group_count):
        tr, tc = i // GC, i % GC
        ok = tr < used
        tile = jnp.where(ok, stage[i], 0.0)
        pad[3 + tr * tile_h : 3 + (tr + 1) * tile_h, edge + tc * tile_w : edge + (tc + 1) * tile_w, :] = tile
    for copy in copies[:3]:
        copy.wait()
    for i in range(group_count):
        tr, tc = i // GC, i % GC
        up = jnp.where(tr < used, cot_ref[i].astype(F32), 0.0)
        upc[tr * tile_h : (tr + 1) * tile_h, tc * tile_w : (tc + 1) * tile_w, :] = up

    block_rows = 8
    for r0 in range(0, height, block_rows):
        for lo, hi in lanes_of:
            acc = jnp.broadcast_to(line(dwb_ref, lo, hi).reshape(1, 1, hi - lo), (block_rows, width, hi - lo))
            for b in range(7):
                part = pad[r0 : r0 + block_rows + 6, edge - 3 + b : edge - 3 + b + width, lo:hi]
                for a in range(7):
                    acc = acc + part[a : a + block_rows] * dwk_ref[a, b : b + 1, lo:hi].reshape(1, 1, hi - lo)
            conv[r0 * width : (r0 + block_rows) * width, lo:hi] = acc.reshape(block_rows * width, hi - lo)

    for copy in copies[3:]:
        copy.wait()

    value = conv[...]
    mean = jnp.mean(value, axis=-1, keepdims=True)
    centered = value - mean
    rstd = lax.rsqrt(jnp.mean(centered * centered, axis=-1, keepdims=True) + 1e-06)
    hat = centered * rstd
    xhat[...] = hat
    rstd_s[...] = jnp.broadcast_to(rstd, rstd_s.shape)
    norm_b[...] = (hat * line(lng_ref) + line(lnb_ref)).astype(BF16)

    row = lax.broadcasted_iota(jnp.int32, (cells, 1), 0)
    mask = (row < used * (tile_h * width)).astype(F32)
    up_f = upc[...].reshape(cells, chans)
    up_b = up_f.astype(BF16)
    normed = norm_b[...]

    total_norm = jnp.zeros((1, 1), F32)
    for h in range(chunks):
        cols = slice(h * LANES, (h + 1) * LANES)
        pre = jnp.dot(normed, win_ref[:, cols], preferred_element_type=F32) + line(bin_ref, cols.start, cols.stop)
        cdf = 0.5 * (1.0 + lax.erf(pre * 0.7071067811865476))
        act = pre * cdf
        pdf = jnp.exp(-0.5 * pre * pre) * 0.3989422804014327
        act_s[:, cols] = act
        gp_s[:, cols] = cdf + pre * pdf
        kept = act * mask
        norm = jnp.sqrt(1.0 + jnp.sum(kept * kept, axis=0, keepdims=True))
        vecs[0:1, cols] = norm
        total_norm = total_norm + jnp.sum(norm, axis=-1, keepdims=True)
        dmix_s[:, cols] = lax.dot_general(
            up_b, wout_ref[:, cols], (((1,), (0,)), ((), ())), preferred_element_type=F32
        )
    den = total_norm / hid + 1e-06

    total_dn = jnp.zeros((1, 1), F32)
    for h in range(chunks):
        cols = slice(h * LANES, (h + 1) * LANES)
        act, dmix = act_s[:, cols], dmix_s[:, cols]
        norm = vecs[0:1, cols]
        scale = norm / den
        gamma = line(gam_ref, cols.start, cols.stop)
        mixed = (gamma * (act * scale) + line(bet_ref, cols.start, cols.stop) + act).astype(BF16)
        mixed_s[:, cols] = mixed
        grad = lax.dot_general(
            mixed, up_b, (((0,), (0,)), ((), ())), preferred_element_type=F32
        )
        for n, (lo, hi) in enumerate(lanes_of):
            wide[n, h * LANES : (h + 1) * LANES, 0 : hi - lo] = grad[:, lo:hi]
        along = jnp.sum(dmix * act, axis=0, keepdims=True)
        vecs[2:3, cols] = along * scale
        vecs[3:4, cols] = jnp.sum(dmix, axis=0, keepdims=True)
        d_scale = along * gamma
        vecs[4:5, cols] = d_scale
        total_dn = total_dn + jnp.sum(d_scale * norm, axis=-1, keepdims=True)
    pull = total_dn / (den * den) / hid

    head = (7 * 7 + 3) * chans // LANES
    for h in range(chunks):
        cols = slice(h * LANES, (h + 1) * LANES)
        act, dmix = act_s[:, cols], dmix_s[:, cols]
        norm = vecs[0:1, cols]
        scale = norm / den
        d_norm = vecs[4:5, cols] / den - pull
        d_act = dmix * (line(gam_ref, cols.start, cols.stop) * scale + 1.0) + act * mask * (d_norm / norm)
        d_pre = d_act * gp_s[:, cols]
        vecs[1:2, cols] = jnp.sum(d_pre, axis=0, keepdims=True)
        d_pre_b = d_pre.astype(BF16)
        dpre_s[:, cols] = d_pre_b
        flat[pl.ds(head + h, chans, stride=chunks), :] = lax.dot_general(
            normed, d_pre_b, (((0,), (0,)), ((), ())), preferred_element_type=F32
        )

    branch = lax.dot_general(
        mixed_s[...], wout_ref[...], (((1,), (1,)), ((), ())), preferred_element_type=F32
    )
    branch = branch + line(bout_ref)
    inner = pad[3 : 3 + height, edge : edge + width, :].reshape(cells, chans)
    conv[...] = jnp.where(mask > 0, inner + branch, 0.0)
    for i in range(group_count):
        tr, tc = i // GC, i % GC
        for a in range(tile_h):
            first = (tr * tile_h + a) * width + tc * tile_w
            out_ref[i, a] = conv[first : first + tile_w, :].astype(BF16)

    d_normed = lax.dot_general(
        dpre_s[...], win_ref[...], (((1,), (1,)), ((), ())), preferred_element_type=F32
    )
    hat = xhat[...]
    put(50, jnp.sum(d_normed * hat, axis=0, keepdims=True))
    put(51, jnp.sum(d_normed, axis=0, keepdims=True))
    e = d_normed * line(lng_ref)
    d_conv = rstd_s[:, 0:1] * (
        e
        - jnp.mean(e, axis=-1, keepdims=True)
        - hat * jnp.mean(e * hat, axis=-1, keepdims=True)
    )
    put(49, jnp.sum(d_conv, axis=0, keepdims=True))
    gpad[3 : 3 + height, edge : edge + width, :] = d_conv.reshape(height, width, chans)

    for n, (lo, hi) in enumerate(lanes_of):
        for b in range(7):
            sums = [None] * 7
            for r0 in range(0, height, block_rows):
                part = pad[r0 : r0 + block_rows + 6, edge - 3 + b : edge - 3 + b + width, lo:hi]
                grad = gpad[3 + r0 : 3 + r0 + block_rows, edge : edge + width, lo:hi]
                for a in range(7):
                    s = jnp.sum(part[a : a + block_rows] * grad, axis=0)
                    sums[a] = s if sums[a] is None else sums[a] + s
            for a in range(7):
                small[n, a * 7 + b : a * 7 + b + 1, 0 : hi - lo] = jnp.sum(sums[a], axis=0, keepdims=True)
        for r0 in range(0, height, block_rows):
            acc = upc[r0 : r0 + block_rows, :, lo:hi]
            for b in range(7):
                part = gpad[r0 : r0 + block_rows + 6, edge + 3 - b : edge + 3 - b + width, lo:hi]
                for a in range(7):
                    acc = acc + part[6 - a : 6 - a + block_rows] * dwk_ref[a, b : b + 1, lo:hi].reshape(1, 1, hi - lo)
            xhat[r0 * width : (r0 + block_rows) * width, lo:hi] = acc.reshape(block_rows * width, hi - lo)
    xhat[...] = jnp.where(mask > 0, xhat[...], 0.0)
    for i in range(group_count):
        tr, tc = i // GC, i % GC
        for a in range(tile_h):
            first = (tr * tile_h + a) * width + tc * tile_w
            for n, (lo, hi) in enumerate(lanes_of):
                at = (n * tile_h + a) * tile_w
                backs[i, at : at + tile_w, 0 : hi - lo] = xhat[first : first + tile_w, lo:hi]
        back_ref[i] = backs[i].astype(BF16)

    store_wide(flat, 0, small, 7 * 7 + 3, chans)
    mid = head + chans * chunks
    for k in range(3):
        for h in range(chunks):
            flat[mid + k * chunks + h : mid + k * chunks + h + 1, :] = vecs[
                1 + k : 2 + k, h * LANES : (h + 1) * LANES
            ]
    late = mid + 3 * chunks
    store_wide(flat, late, wide, hid, chans)
    tail = late + chans * chunks
    flat[tail : plan.flat_rows, :] = jnp.zeros((plan.flat_rows - tail, LANES), F32)
    g_bias_out = jnp.sum(up_f, axis=0, keepdims=True)
    for n, (lo, hi) in enumerate(lanes_of):
        flat[tail + n : tail + n + 1, 0 : hi - lo] = g_bias_out[:, lo:hi]

    dlo = d % plan.core

    def cut(j, carry):
        dhi, rest = j // plan.ng, j % plan.ng
        mine = (dhi * plan.core + dlo) * plan.ng + rest
        keep_ref[j] = flat[pl.ds((mine * plan.shard) // LANES, plan.rows), :]
        if plan.core > 1:
            other = (dhi * plan.core + (1 - dlo)) * plan.ng + rest
            send_ref[j] = flat[pl.ds((other * plan.shard) // LANES, plan.rows), :].astype(BF16)
        return carry

    lax.fori_loop(0, plan.blocks, cut, 0)


def cube_kernel(plan, keep_ref, recv_ref, back_ref, own_ref, *send_refs):
    dhi, _, _, glo = plan.digits(lax.axis_index("dp"), lax.axis_index("group"))
    tile_rows = back_ref.shape[1]
    for m in range(plan.cube):
        to_d = partner(dhi, m // plan.glo, plan.dhi)[0]
        to_g = partner(glo, m % plan.glo, plan.glo)[0]
        for q in range(plan.ghi):
            j = to_d * plan.ng + q * plan.glo + to_g
            value = keep_ref[j]
            if plan.core > 1:
                value = value + recv_ref[j].astype(F32)
            if m == 0:
                own_ref[q] = value
                continue
            ref = send_refs[m - 1]
            ref[q * plan.rows : (q + 1) * plan.rows] = value.astype(BF16)
            if m < plan.glo:
                at = plan.ghi * plan.rows + q * tile_rows
                ref[at : at + tile_rows] = back_ref[q * plan.glo + to_g]


def high_kernel(plan, keep_ref, back_ref, *refs):
    recv_refs = refs[: plan.cube - 1]
    own_ref, tiles_ref = refs[plan.cube - 1 : plan.cube + 1]
    send_refs = refs[plan.cube + 1 :]
    _, _, ghi, glo = plan.digits(lax.axis_index("dp"), lax.axis_index("group"))
    tile_rows = back_ref.shape[1]
    for r in range(plan.ghi):
        q = partner(ghi, r, plan.ghi)[0]
        value = keep_ref[q]
        for ref in recv_refs:
            value = value + ref[pl.ds(pl.multiple_of(q * plan.rows, 16), plan.rows), :].astype(F32)
        if r == 0:
            own_ref[...] = value
        else:
            send_refs[r - 1][0 : plan.rows] = value.astype(BF16)
        for n in range(plan.glo):
            if n == 0:
                tile = back_ref[q * plan.glo + glo]
            else:
                at = pl.multiple_of(plan.ghi * plan.rows + q * tile_rows, 16)
                tile = recv_refs[n - 1][pl.ds(at, tile_rows), :]
            if r == 0:
                tiles_ref[n] = tile
            else:
                at = plan.rows + n * tile_rows
                send_refs[r - 1][at : at + tile_rows] = tile


def last_kernel(plan, factor, keep_ref, tiles_ref, *refs):
    recv_refs = refs[: plan.ghi - 1]
    out_ref, grads_ref, total = refs[plan.ghi - 1 :]
    d, g = lax.axis_index("dp"), lax.axis_index("group")
    _, _, ghi, glo = plan.digits(d, g)
    _, tile_h, tile_w, chans = grads_ref.shape
    tile_rows = tiles_ref.shape[1]
    value = keep_ref[...]
    for ref in recv_refs:
        value = value + ref[0 : plan.rows].astype(F32)
    shift = ((d * plan.ng + g) * plan.shard) % LANES
    lane = lax.broadcasted_iota(jnp.int32, (1, LANES), 1)
    total[0 : plan.rows, :] = pltpu.roll(value * factor, LANES - shift, 1)
    count = out_ref.shape[0]
    out_ref[...] = jnp.where(
        lane < LANES - shift, total[0:count, :], total[1 : count + 1, :]
    )
    for r in range(plan.ghi):
        for n in range(plan.glo):
            source = partner(ghi, r, plan.ghi)[1] * plan.glo + partner(glo, n, plan.glo)[1]
            if r == 0:
                tile = tiles_ref[n]
            else:
                at = plan.rows + n * tile_rows
                tile = recv_refs[r - 1][at : at + tile_rows]
            tile = tile.astype(F32)
            for k, lo in enumerate(range(0, chans, LANES)):
                hi = min(lo + LANES, chans)
                for a in range(tile_h):
                    at = (k * tile_h + a) * tile_w
                    grads_ref[source, a, :, lo:hi] = tile[at : at + tile_w, 0 : hi - lo].astype(BF16)


VM = pl.BlockSpec(memory_space=pltpu.VMEM)
SM = pl.BlockSpec(memory_space=pltpu.SMEM)


HB = pl.BlockSpec(memory_space=pltpu.HBM)


def call(kernel, inputs, out_shapes, scratch=(), name=None, specs=None, limit=12):
    return pl.pallas_call(
        kernel,
        in_specs=specs or [VM] * len(inputs),
        out_specs=[VM] * len(out_shapes),
        out_shape=out_shapes,
        scratch_shapes=list(scratch),
        compiler_params=pltpu.CompilerParams(vmem_limit_bytes=limit << 20),
        name=name,
    )(*inputs)


def per_device(
    image_tiles, cotangent, image_rows, dw_kernel, dw_bias, layer_norm_gain, layer_norm_bias,
    weight_in, bias_in, grn_gamma, grn_beta, weight_out, bias_out,
):
    axes = ("dp", "group")
    nd, ng = lax.axis_size("dp"), lax.axis_size("group")
    tiles = image_tiles[0, 0]
    _, tile_h, tile_w, chans = tiles.shape
    hid = weight_in.shape[1]
    total_len = 49 * chans + 3 * chans + 2 * chans * hid + 3 * hid + chans
    plan = Plan(nd, ng, total_len)
    height, width = (ng // GC) * tile_h, GC * tile_w
    cells = height * width

    tile = (tile_h, tile_w, chans)
    own, *sends = call(
        functools.partial(pick_kernel, plan),
        (pltpu.with_memory_space_constraint(tiles, pltpu.HBM),),
        [jax.ShapeDtypeStruct((plan.ghi, *tile), BF16)] * plan.glo,
        [pltpu.SemaphoreType.DMA((ng,))],
        name="pick",
        specs=[HB],
    )
    recvs = [
        lax.ppermute(x, axes, plan.pairs(cube_step=n + 1)) for n, x in enumerate(sends)
    ]
    own, *sends = call(
        functools.partial(turn_kernel, plan),
        (own, *recvs),
        [jax.ShapeDtypeStruct((plan.glo, *tile), BF16)] * plan.ghi,
        name="turn",
    )
    recvs = [
        lax.ppermute(x, axes, plan.pairs(high_step=r + 1)) for r, x in enumerate(sends)
    ]

    block = (plan.rows, LANES)
    wide = -(-chans // LANES)
    tile_rows = wide * tile_h * tile_w
    back_shape = jax.ShapeDtypeStruct((ng, tile_rows, LANES), BF16)
    params = (
        dw_kernel, dw_bias, cotangent[0, 0], layer_norm_gain, layer_norm_bias, weight_in,
        bias_in, weight_out.T, grn_gamma, grn_beta, bias_out,
    )
    outputs, backs, keep, send = call(
        functools.partial(image_kernel, plan),
        (
            image_rows, own, *recvs,
            *[pltpu.with_memory_space_constraint(p, pltpu.HBM) for p in params],
        ),
        [
            jax.ShapeDtypeStruct(tiles.shape, BF16),
            back_shape,
            jax.ShapeDtypeStruct((plan.blocks, *block), F32),
            jax.ShapeDtypeStruct((plan.blocks, *block), BF16),
        ],
        [pltpu.VMEM(p.shape, p.dtype) for p in params]
        + [
            pltpu.SemaphoreType.DMA((PARAMS,)),
            pltpu.VMEM((ng, *tile), F32),
            pltpu.VMEM((height + 6, width + 16, chans), F32),
            pltpu.VMEM((height, width, chans), F32),
            pltpu.VMEM((cells, chans), F32),
            pltpu.VMEM((cells, chans), F32),
            pltpu.VMEM((cells, LANES), F32),
            pltpu.VMEM((cells, chans), BF16),
            pltpu.VMEM((cells, hid), F32),
            pltpu.VMEM((cells, hid), F32),
            pltpu.VMEM((cells, hid), F32),
            pltpu.VMEM((cells, hid), BF16),
            pltpu.VMEM((cells, hid), BF16),
            pltpu.VMEM((8, hid), F32),
            pltpu.VMEM((wide, hid, LANES), F32),
            pltpu.VMEM((wide, 56, LANES), F32),
            pltpu.VMEM((height + 6, width + 16, chans), F32),
            pltpu.VMEM((ng, tile_rows, LANES), F32),
            pltpu.VMEM((plan.flat_rows, LANES), F32),
        ],
        name="image",
        specs=[SM] + [VM] * plan.ghi + [HB] * PARAMS,
        limit=40,
    )

    recv = lax.ppermute(send, axes, plan.pairs(core_step=1)) if plan.core > 1 else send
    count = plan.ghi * plan.rows
    own, *sends = call(
        functools.partial(cube_kernel, plan),
        (keep, recv, backs),
        [jax.ShapeDtypeStruct((plan.ghi, *block), F32)]
        + [
            jax.ShapeDtypeStruct(
                (count + (plan.ghi * tile_rows if m < plan.glo else 0), LANES), BF16
            )
            for m in range(1, plan.cube)
        ],
        name="cube",
    )
    recvs = [None] * len(sends)
    for m in plan.order():
        recvs[m - 1] = lax.ppermute(sends[m - 1], axes, plan.pairs(cube_step=m))
    own, held, *sends = call(
        functools.partial(high_kernel, plan),
        (own, backs, *recvs),
        [
            jax.ShapeDtypeStruct(block, F32),
            jax.ShapeDtypeStruct((plan.glo, tile_rows, LANES), BF16),
        ]
        + [jax.ShapeDtypeStruct((plan.rows + plan.glo * tile_rows, LANES), BF16)]
        * (plan.ghi - 1),
        name="high",
    )
    recvs = [
        lax.ppermute(x, axes, plan.pairs(high_step=r + 1)) for r, x in enumerate(sends)
    ]
    factor = 1.0 / math.sqrt(nd * ng * ng * tile_h * tile_w)
    out_rows = -(-plan.shard // LANES)
    shard, grads = call(
        functools.partial(last_kernel, plan, factor),
        (own, held, *recvs),
        [
            jax.ShapeDtypeStruct((out_rows, LANES), F32),
            jax.ShapeDtypeStruct(tiles.shape, BF16),
        ],
        [pltpu.VMEM((plan.rows + 8, LANES), F32)],
        name="last",
    )
    shard = shard.reshape(1, -1)[:, : plan.shard]
    return (outputs[None, None], grads[None, None], shard)


def solution(mesh):
    tiled = P("dp", "group", None, None, None, None)
    return jax.shard_map(
        per_device,
        mesh=mesh,
        in_specs=(tiled, tiled, P("dp", "group")) + (P(),) * 10,
        out_specs=(tiled, tiled, P(("dp", "group"), None)),
        check_vma=False,
    )
```

```python
import math
import functools

import jax
import jax.numpy as jnp
from jax import lax
from jax.experimental import pallas as pl
from jax.experimental.pallas import tpu as pltpu
from jax.sharding import PartitionSpec as P

GC = 4
SMALL = 9
LANES = 128
F32 = jnp.float32
BF16 = jnp.bfloat16


def partner(digit, step, count):
    if count & (count - 1) == 0:
        return digit ^ step, digit ^ step
    return (digit + step) % count, (digit + count - step) % count


class Plan:
    def __init__(self, data_count, group_count, total_len):
        self.nd, self.ng = data_count, group_count
        self.devices = data_count * group_count
        self.shard = (total_len + 8 * self.devices - 1) // (8 * self.devices) * 8
        self.rows = -(-(self.shard + LANES - 1) // LANES)
        self.rows = -(-self.rows // 16) * 16
        self.core = math.gcd(data_count, 2)
        self.dhi = data_count // self.core
        self.glo = math.gcd(group_count, 4)
        self.ghi = group_count // self.glo
        self.blocks = self.dhi * group_count
        self.cube = self.dhi * self.glo
        last = ((self.devices - 1) * self.shard) // LANES + self.rows
        self.flat_rows = -(-max(last, -(-total_len // LANES)) // 8) * 8

    def digits(self, d, g):
        return d // self.core, d % self.core, g // self.glo, g % self.glo

    def device(self, dhi, dlo, ghi, glo):
        return (dhi * self.core + dlo) * self.ng + ghi * self.glo + glo

    def order(self):
        def far(m):
            high, low = m // self.glo, m % self.glo
            return ((high > 0) + bin(low).count("1"), high == 0, m)

        return sorted(range(1, self.cube), key=far)

    def pairs(self, core_step=0, cube_step=0, high_step=0):
        out = []
        for d in range(self.nd):
            for g in range(self.ng):
                dhi, dlo, ghi, glo = self.digits(d, g)
                to = self.device(
                    partner(dhi, cube_step // self.glo, self.dhi)[0],
                    partner(dlo, core_step, self.core)[0],
                    partner(ghi, high_step, self.ghi)[0],
                    partner(glo, cube_step % self.glo, self.glo)[0],
                )
                out.append((d * self.ng + g, to))
        return out


def pick_kernel(plan, tiles_ref, *refs):
    sources, out_refs, sems = refs[:SMALL], refs[SMALL:-1], refs[-1]
    out_refs, held = out_refs[: plan.glo], out_refs[plan.glo :]
    glo = lax.axis_index("group") % plan.glo
    copies = []
    for n, ref in enumerate(out_refs):
        to = partner(glo, n, plan.glo)[0]
        for q in range(plan.ghi):
            copies.append(
                pltpu.make_async_copy(
                    tiles_ref.at[q * plan.glo + to], ref.at[q], sems.at[n * plan.ghi + q]
                )
            )
    for n, (source, ref) in enumerate(zip(sources, held)):
        copies.append(pltpu.make_async_copy(source, ref, sems.at[plan.ng + n]))
    for copy in copies:
        copy.start()
    for copy in copies:
        copy.wait()


def turn_kernel(plan, *refs):
    in_refs, out_refs = refs[: plan.glo], refs[plan.glo :]
    ghi = lax.axis_index("group") // plan.glo
    for r, ref in enumerate(out_refs):
        q = partner(ghi, r, plan.ghi)[0]
        for n in range(plan.glo):
            ref[n] = in_refs[n][q]


def store_wide(flat_ref, base, src_ref, rows, width):
    unit = LANES // math.gcd(width, LANES)
    groups = rows // unit
    per_group = unit * width // LANES
    lane = lax.broadcasted_iota(jnp.int32, (1, LANES), 1)
    step = 88
    for first in range(0, groups, step):
        count = min(step, groups - first)
        for block in range(per_group):
            begin, end = block * LANES, (block + 1) * LANES
            value = None
            for t in range(unit):
                lo, hi = max(begin, t * width), min(end, (t + 1) * width)
                if lo >= hi:
                    continue
                shift = (t * width) % LANES
                at = lo
                while at < hi:
                    piece = (at - t * width) // LANES
                    stop = min(hi, t * width + (piece + 1) * LANES)
                    part = src_ref[piece, pl.ds(t + unit * first, count, stride=unit), :]
                    if shift:
                        part = pltpu.roll(part, shift, 1)
                    if value is None:
                        value = part
                    else:
                        value = jnp.where(lane >= at - begin, part, value)
                    at = stop
            flat_ref[pl.ds(base + block + per_group * first, count, stride=per_group), :] = value


def image_kernel(
    plan,
    rows_ref,
    *refs,
):
    group_count = plan.ng
    recv_refs, refs = refs[: plan.ghi], refs[plan.ghi :]
    (
        dwk_ref, dwb_ref, cot_ref, lng_ref, lnb_ref, bin_ref, gam_ref, bet_ref, bout_ref,
    ) = refs[:SMALL]
    win_hbm, wout_hbm, out_hbm, upc, gpad, keep_ref, send_ref = refs[SMALL : SMALL + 7]
    (
        win_ref, wout_ref, out_ref, sems, stage, pad, shifted, conv, xhat, rstd_s, norm_b,
        act_s, gp_s, dmix_s, mixed_s, dpre_s, vecs, wide, small, flat,
    ) = refs[SMALL + 7 :]
    weights = [
        pltpu.make_async_copy(win_hbm, win_ref, sems.at[0]),
        pltpu.make_async_copy(wout_hbm, wout_ref, sems.at[1]),
    ]
    store_out = pltpu.make_async_copy(out_ref, out_hbm, sems.at[2])
    for copy in weights:
        copy.start()
    d, g, used = lax.axis_index("dp"), lax.axis_index("group"), rows_ref[0, 0]
    _, _, ghi, glo = plan.digits(d, g)
    _, tile_h, tile_w, chans = recv_refs[0].shape
    hid = win_ref.shape[1]
    grid_rows = group_count // GC
    height, width = grid_rows * tile_h, GC * tile_w
    cells = height * width
    edge = 8
    lanes_of = [(lo, min(lo + LANES, chans)) for lo in range(0, chans, LANES)]
    chunks = hid // LANES

    def line(ref, lo=0, hi=None):
        hi = ref.shape[0] if hi is None else hi
        return ref[lo:hi].reshape(1, hi - lo)

    def put(at, sums):
        for n, (lo, hi) in enumerate(lanes_of):
            small[n, at : at + 1, 0 : hi - lo] = sums[:, lo:hi]

    for r, ref in enumerate(recv_refs):
        for n in range(plan.glo):
            source = partner(ghi, r, plan.ghi)[1] * plan.glo + partner(glo, n, plan.glo)[1]
            stage[source] = ref[n].astype(F32)
    pad[...] = jnp.zeros_like(pad)
    gpad[...] = jnp.zeros_like(gpad)
    for i in range(group_count):
        tr, tc = i // GC, i % GC
        ok = tr < used
        tile = jnp.where(ok, stage[i], 0.0)
        pad[3 + tr * tile_h : 3 + (tr + 1) * tile_h, edge + tc * tile_w : edge + (tc + 1) * tile_w, :] = tile
    for i in range(group_count):
        tr, tc = i // GC, i % GC
        up = jnp.where(tr < used, cot_ref[i].astype(F32), 0.0)
        upc[tr * tile_h : (tr + 1) * tile_h, tc * tile_w : (tc + 1) * tile_w, :] = up

    block_rows = 8
    for r0 in range(0, height, block_rows):
        for lo, hi in lanes_of:
            acc = jnp.broadcast_to(line(dwb_ref, lo, hi).reshape(1, 1, hi - lo), (block_rows, width, hi - lo))
            for b in range(7):
                part = pad[r0 : r0 + block_rows + 6, edge - 3 + b : edge - 3 + b + width, lo:hi]
                shifted[b, r0 : r0 + block_rows + 6, :, lo:hi] = part
                for a in range(7):
                    acc = acc + part[a : a + block_rows] * dwk_ref[a, b : b + 1, lo:hi].reshape(1, 1, hi - lo)
            conv[r0 * width : (r0 + block_rows) * width, lo:hi] = acc.reshape(block_rows * width, hi - lo)

    for copy in weights:
        copy.wait()

    value = conv[...]
    mean = jnp.mean(value, axis=-1, keepdims=True)
    centered = value - mean
    rstd = lax.rsqrt(jnp.mean(centered * centered, axis=-1, keepdims=True) + 1e-06)
    hat = centered * rstd
    xhat[...] = hat
    rstd_s[...] = jnp.broadcast_to(rstd, rstd_s.shape)
    norm_b[...] = (hat * line(lng_ref) + line(lnb_ref)).astype(BF16)

    row = lax.broadcasted_iota(jnp.int32, (cells, 1), 0)
    mask = (row < used * (tile_h * width)).astype(F32)
    up_f = upc[...].reshape(cells, chans)
    up_b = up_f.astype(BF16)
    normed = norm_b[...]

    total_norm = jnp.zeros((1, 1), F32)
    for h in range(chunks):
        cols = slice(h * LANES, (h + 1) * LANES)
        pre = jnp.dot(normed, win_ref[:, cols], preferred_element_type=F32) + line(bin_ref, cols.start, cols.stop)
        cdf = 0.5 * (1.0 + lax.erf(pre * 0.7071067811865476))
        act = pre * cdf
        pdf = jnp.exp(-0.5 * pre * pre) * 0.3989422804014327
        act_s[:, cols] = act
        gp_s[:, cols] = cdf + pre * pdf
        kept = act * mask
        norm = jnp.sqrt(1.0 + jnp.sum(kept * kept, axis=0, keepdims=True))
        vecs[0:1, cols] = norm
        total_norm = total_norm + jnp.sum(norm, axis=-1, keepdims=True)
        dmix_s[:, cols] = lax.dot_general(
            up_b, wout_ref[:, cols], (((1,), (0,)), ((), ())), preferred_element_type=F32
        )
    den = total_norm / hid + 1e-06

    total_dn = jnp.zeros((1, 1), F32)
    for h in range(chunks):
        cols = slice(h * LANES, (h + 1) * LANES)
        act, dmix = act_s[:, cols], dmix_s[:, cols]
        norm = vecs[0:1, cols]
        scale = norm / den
        gamma = line(gam_ref, cols.start, cols.stop)
        mixed = (gamma * (act * scale) + line(bet_ref, cols.start, cols.stop) + act).astype(BF16)
        mixed_s[:, cols] = mixed
        grad = lax.dot_general(
            mixed, up_b, (((0,), (0,)), ((), ())), preferred_element_type=F32
        )
        for n, (lo, hi) in enumerate(lanes_of):
            wide[n, h * LANES : (h + 1) * LANES, 0 : hi - lo] = grad[:, lo:hi]
        along = jnp.sum(dmix * act, axis=0, keepdims=True)
        vecs[2:3, cols] = along * scale
        vecs[3:4, cols] = jnp.sum(dmix, axis=0, keepdims=True)
        d_scale = along * gamma
        vecs[4:5, cols] = d_scale
        total_dn = total_dn + jnp.sum(d_scale * norm, axis=-1, keepdims=True)
    pull = total_dn / (den * den) / hid

    head = (7 * 7 + 3) * chans // LANES
    for h in range(chunks):
        cols = slice(h * LANES, (h + 1) * LANES)
        act, dmix = act_s[:, cols], dmix_s[:, cols]
        norm = vecs[0:1, cols]
        scale = norm / den
        d_norm = vecs[4:5, cols] / den - pull
        d_act = dmix * (line(gam_ref, cols.start, cols.stop) * scale + 1.0) + act * mask * (d_norm / norm)
        d_pre = d_act * gp_s[:, cols]
        vecs[1:2, cols] = jnp.sum(d_pre, axis=0, keepdims=True)
        d_pre_b = d_pre.astype(BF16)
        dpre_s[:, cols] = d_pre_b
        flat[pl.ds(head + h, chans, stride=chunks), :] = lax.dot_general(
            normed, d_pre_b, (((0,), (0,)), ((), ())), preferred_element_type=F32
        )

    branch = lax.dot_general(
        mixed_s[...], wout_ref[...], (((1,), (1,)), ((), ())), preferred_element_type=F32
    )
    branch = branch + line(bout_ref)
    inner = pad[3 : 3 + height, edge : edge + width, :].reshape(cells, chans)
    conv[...] = jnp.where(mask > 0, inner + branch, 0.0)
    for i in range(group_count):
        tr, tc = i // GC, i % GC
        for a in range(tile_h):
            first = (tr * tile_h + a) * width + tc * tile_w
            out_ref[i, a] = conv[first : first + tile_w, :].astype(BF16)
    store_out.start()

    d_normed = lax.dot_general(
        dpre_s[...], win_ref[...], (((1,), (1,)), ((), ())), preferred_element_type=F32
    )
    hat = xhat[...]
    put(50, jnp.sum(d_normed * hat, axis=0, keepdims=True))
    put(51, jnp.sum(d_normed, axis=0, keepdims=True))
    e = d_normed * line(lng_ref)
    d_conv = rstd_s[:, 0:1] * (
        e
        - jnp.mean(e, axis=-1, keepdims=True)
        - hat * jnp.mean(e * hat, axis=-1, keepdims=True)
    )
    put(49, jnp.sum(d_conv, axis=0, keepdims=True))
    gpad[3 : 3 + height, edge : edge + width, :] = d_conv.reshape(height, width, chans)

    for n, (lo, hi) in enumerate(lanes_of):
        for b in range(7):
            sums = [None] * 7
            for r0 in range(0, height, block_rows):
                part = shifted[b, r0 : r0 + block_rows + 6, :, lo:hi]
                grad = gpad[3 + r0 : 3 + r0 + block_rows, edge : edge + width, lo:hi]
                for a in range(7):
                    s = jnp.sum(part[a : a + block_rows] * grad, axis=0)
                    sums[a] = s if sums[a] is None else sums[a] + s
            for a in range(7):
                small[n, a * 7 + b : a * 7 + b + 1, 0 : hi - lo] = jnp.sum(sums[a], axis=0, keepdims=True)

    store_wide(flat, 0, small, 7 * 7 + 3, chans)
    mid = head + chans * chunks
    for k in range(3):
        for h in range(chunks):
            flat[mid + k * chunks + h : mid + k * chunks + h + 1, :] = vecs[
                1 + k : 2 + k, h * LANES : (h + 1) * LANES
            ]
    late = mid + 3 * chunks
    store_wide(flat, late, wide, hid, chans)
    tail = late + chans * chunks
    flat[tail : plan.flat_rows, :] = jnp.zeros((plan.flat_rows - tail, LANES), F32)
    g_bias_out = jnp.sum(up_f, axis=0, keepdims=True)
    for n, (lo, hi) in enumerate(lanes_of):
        flat[tail + n : tail + n + 1, 0 : hi - lo] = g_bias_out[:, lo:hi]

    dlo = d % plan.core

    def cut(j, carry):
        dhi, rest = j // plan.ng, j % plan.ng
        mine = (dhi * plan.core + dlo) * plan.ng + rest
        keep_ref[j] = flat[pl.ds((mine * plan.shard) // LANES, plan.rows), :]
        if plan.core > 1:
            other = (dhi * plan.core + (1 - dlo)) * plan.ng + rest
            send_ref[j] = flat[pl.ds((other * plan.shard) // LANES, plan.rows), :].astype(BF16)
        return carry

    lax.fori_loop(0, plan.blocks, cut, 0)
    store_out.wait()


def back_kernel(plan, rows_ref, dwk_ref, upc, gpad, back_ref, total, backs):
    used = rows_ref[0, 0]
    height, width, chans = upc.shape
    tile_w = width // GC
    tile_h = height * GC // plan.ng
    edge, block_rows = 8, 8
    lanes_of = [(lo, min(lo + LANES, chans)) for lo in range(0, chans, LANES)]
    for lo, hi in lanes_of:
        for r0 in range(0, height, block_rows):
            acc = upc[r0 : r0 + block_rows, :, lo:hi]
            for b in range(7):
                part = gpad[r0 : r0 + block_rows + 6, edge + 3 - b : edge + 3 - b + width, lo:hi]
                for a in range(7):
                    acc = acc + part[6 - a : 6 - a + block_rows] * dwk_ref[a, b : b + 1, lo:hi].reshape(1, 1, hi - lo)
            total[r0 * width : (r0 + block_rows) * width, lo:hi] = acc.reshape(block_rows * width, hi - lo)
    for i in range(plan.ng):
        tr, tc = i // GC, i % GC
        for a in range(tile_h):
            first = (tr * tile_h + a) * width + tc * tile_w
            for n, (lo, hi) in enumerate(lanes_of):
                at = (n * tile_h + a) * tile_w
                backs[i, at : at + tile_w, 0 : hi - lo] = jnp.where(
                    tr < used, total[first : first + tile_w, lo:hi], 0.0
                )
        back_ref[i] = backs[i].astype(BF16)


def cube_kernel(plan, keep_ref, recv_ref, back_ref, own_ref, *send_refs):
    dhi, _, _, glo = plan.digits(lax.axis_index("dp"), lax.axis_index("group"))
    tile_rows = back_ref.shape[1]
    for m in range(plan.cube):
        to_d = partner(dhi, m // plan.glo, plan.dhi)[0]
        to_g = partner(glo, m % plan.glo, plan.glo)[0]
        for q in range(plan.ghi):
            j = to_d * plan.ng + q * plan.glo + to_g
            value = keep_ref[j]
            if plan.core > 1:
                value = value + recv_ref[j].astype(F32)
            if m == 0:
                own_ref[q] = value
                continue
            ref = send_refs[m - 1]
            ref[q * plan.rows : (q + 1) * plan.rows] = value.astype(BF16)
            if m < plan.glo:
                at = plan.ghi * plan.rows + q * tile_rows
                ref[at : at + tile_rows] = back_ref[q * plan.glo + to_g]


def high_kernel(plan, keep_ref, back_ref, *refs):
    recv_refs = refs[: plan.cube - 1]
    own_ref, tiles_ref = refs[plan.cube - 1 : plan.cube + 1]
    send_refs = refs[plan.cube + 1 :]
    _, _, ghi, glo = plan.digits(lax.axis_index("dp"), lax.axis_index("group"))
    tile_rows = back_ref.shape[1]
    for r in range(plan.ghi):
        q = partner(ghi, r, plan.ghi)[0]
        value = keep_ref[q]
        for ref in recv_refs:
            value = value + ref[pl.ds(pl.multiple_of(q * plan.rows, 16), plan.rows), :].astype(F32)
        if r == 0:
            own_ref[...] = value
        else:
            send_refs[r - 1][0 : plan.rows] = value.astype(BF16)
        for n in range(plan.glo):
            if n == 0:
                tile = back_ref[q * plan.glo + glo]
            else:
                at = pl.multiple_of(plan.ghi * plan.rows + q * tile_rows, 16)
                tile = recv_refs[n - 1][pl.ds(at, tile_rows), :]
            if r == 0:
                tiles_ref[n] = tile
            else:
                at = plan.rows + n * tile_rows
                send_refs[r - 1][at : at + tile_rows] = tile


def last_kernel(plan, factor, keep_ref, tiles_ref, *refs):
    recv_refs = refs[: plan.ghi - 1]
    out_ref, grads_ref, total = refs[plan.ghi - 1 :]
    d, g = lax.axis_index("dp"), lax.axis_index("group")
    _, _, ghi, glo = plan.digits(d, g)
    _, tile_h, tile_w, chans = grads_ref.shape
    tile_rows = tiles_ref.shape[1]
    value = keep_ref[...]
    for ref in recv_refs:
        value = value + ref[0 : plan.rows].astype(F32)
    shift = ((d * plan.ng + g) * plan.shard) % LANES
    lane = lax.broadcasted_iota(jnp.int32, (1, LANES), 1)
    total[0 : plan.rows, :] = pltpu.roll(value * factor, LANES - shift, 1)
    count = out_ref.shape[0]
    out_ref[...] = jnp.where(
        lane < LANES - shift, total[0:count, :], total[1 : count + 1, :]
    )
    for r in range(plan.ghi):
        for n in range(plan.glo):
            source = partner(ghi, r, plan.ghi)[1] * plan.glo + partner(glo, n, plan.glo)[1]
            if r == 0:
                tile = tiles_ref[n]
            else:
                at = plan.rows + n * tile_rows
                tile = recv_refs[r - 1][at : at + tile_rows]
            tile = tile.astype(F32)
            for k, lo in enumerate(range(0, chans, LANES)):
                hi = min(lo + LANES, chans)
                for a in range(tile_h):
                    at = (k * tile_h + a) * tile_w
                    grads_ref[source, a, :, lo:hi] = tile[at : at + tile_w, 0 : hi - lo].astype(BF16)


VM = pl.BlockSpec(memory_space=pltpu.VMEM)
SM = pl.BlockSpec(memory_space=pltpu.SMEM)


HB = pl.BlockSpec(memory_space=pltpu.HBM)


def call(kernel, inputs, out_shapes, scratch=(), name=None, specs=None, out_specs=None, limit=12):
    return pl.pallas_call(
        kernel,
        in_specs=specs or [VM] * len(inputs),
        out_specs=out_specs or [VM] * len(out_shapes),
        out_shape=out_shapes,
        scratch_shapes=list(scratch),
        compiler_params=pltpu.CompilerParams(vmem_limit_bytes=limit << 20),
        name=name,
    )(*inputs)


def per_device(
    image_tiles, cotangent, image_rows, dw_kernel, dw_bias, layer_norm_gain, layer_norm_bias,
    weight_in, bias_in, grn_gamma, grn_beta, weight_out, bias_out,
):
    axes = ("dp", "group")
    nd, ng = lax.axis_size("dp"), lax.axis_size("group")
    tiles = image_tiles[0, 0]
    _, tile_h, tile_w, chans = tiles.shape
    hid = weight_in.shape[1]
    total_len = 49 * chans + 3 * chans + 2 * chans * hid + 3 * hid + chans
    plan = Plan(nd, ng, total_len)
    height, width = (ng // GC) * tile_h, GC * tile_w
    cells = height * width

    tile = (tile_h, tile_w, chans)
    small = (
        dw_kernel, dw_bias, cotangent[0, 0], layer_norm_gain, layer_norm_bias, bias_in,
        grn_gamma, grn_beta, bias_out,
    )
    far = lambda x: pltpu.with_memory_space_constraint(x, pltpu.HBM)
    picked = call(
        functools.partial(pick_kernel, plan),
        (far(tiles), *map(far, small)),
        [jax.ShapeDtypeStruct((plan.ghi, *tile), BF16)] * plan.glo
        + [jax.ShapeDtypeStruct(p.shape, p.dtype) for p in small],
        [pltpu.SemaphoreType.DMA((ng + SMALL,))],
        name="pick",
        specs=[HB] * (1 + SMALL),
    )
    own, sends, small = picked[0], picked[1 : plan.glo], picked[plan.glo :]
    recvs = [
        lax.ppermute(x, axes, plan.pairs(cube_step=n + 1)) for n, x in enumerate(sends)
    ]
    own, *sends = call(
        functools.partial(turn_kernel, plan),
        (own, *recvs),
        [jax.ShapeDtypeStruct((plan.glo, *tile), BF16)] * plan.ghi,
        name="turn",
    )
    recvs = [
        lax.ppermute(x, axes, plan.pairs(high_step=r + 1)) for r, x in enumerate(sends)
    ]

    block = (plan.rows, LANES)
    wide = -(-chans // LANES)
    tile_rows = wide * tile_h * tile_w
    outputs, upc, gpad, keep, send = call(
        functools.partial(image_kernel, plan),
        (image_rows, own, *recvs, *small, far(weight_in), far(weight_out.T)),
        [
            jax.ShapeDtypeStruct(tiles.shape, BF16),
            jax.ShapeDtypeStruct((height, width, chans), F32),
            jax.ShapeDtypeStruct((height + 6, width + 16, chans), F32),
            jax.ShapeDtypeStruct((plan.blocks, *block), F32),
            jax.ShapeDtypeStruct((plan.blocks, *block), BF16),
        ],
        [
            pltpu.VMEM((chans, hid), BF16),
            pltpu.VMEM((chans, hid), BF16),
            pltpu.VMEM(tiles.shape, BF16),
            pltpu.SemaphoreType.DMA((3,)),
            pltpu.VMEM((ng, *tile), F32),
            pltpu.VMEM((height + 6, width + 16, chans), F32),
            pltpu.VMEM((7, height + 6, width, chans), F32),
            pltpu.VMEM((cells, chans), F32),
            pltpu.VMEM((cells, chans), F32),
            pltpu.VMEM((cells, LANES), F32),
            pltpu.VMEM((cells, chans), BF16),
            pltpu.VMEM((cells, hid), F32),
            pltpu.VMEM((cells, hid), F32),
            pltpu.VMEM((cells, hid), F32),
            pltpu.VMEM((cells, hid), BF16),
            pltpu.VMEM((cells, hid), BF16),
            pltpu.VMEM((8, hid), F32),
            pltpu.VMEM((wide, hid, LANES), F32),
            pltpu.VMEM((wide, 56, LANES), F32),
            pltpu.VMEM((plan.flat_rows, LANES), F32),
        ],
        name="image",
        specs=[SM] + [VM] * (plan.ghi + SMALL) + [HB] * 2,
        out_specs=[HB] + [VM] * 4,
        limit=44,
    )
    (backs,) = call(
        functools.partial(back_kernel, plan),
        (image_rows, small[0], upc, gpad),
        [jax.ShapeDtypeStruct((ng, tile_rows, LANES), BF16)],
        [
            pltpu.VMEM((cells, chans), F32),
            pltpu.VMEM((ng, tile_rows, LANES), F32),
        ],
        name="back",
        specs=[SM] + [VM] * 3,
        limit=16,
    )

    recv = lax.ppermute(send, axes, plan.pairs(core_step=1)) if plan.core > 1 else send
    count = plan.ghi * plan.rows
    own, *sends = call(
        functools.partial(cube_kernel, plan),
        (keep, recv, backs),
        [jax.ShapeDtypeStruct((plan.ghi, *block), F32)]
        + [
            jax.ShapeDtypeStruct(
                (count + (plan.ghi * tile_rows if m < plan.glo else 0), LANES), BF16
            )
            for m in range(1, plan.cube)
        ],
        name="cube",
    )
    recvs = [None] * len(sends)
    for m in plan.order():
        recvs[m - 1] = lax.ppermute(sends[m - 1], axes, plan.pairs(cube_step=m))
    own, held, *sends = call(
        functools.partial(high_kernel, plan),
        (own, backs, *recvs),
        [
            jax.ShapeDtypeStruct(block, F32),
            jax.ShapeDtypeStruct((plan.glo, tile_rows, LANES), BF16),
        ]
        + [jax.ShapeDtypeStruct((plan.rows + plan.glo * tile_rows, LANES), BF16)]
        * (plan.ghi - 1),
        name="high",
    )
    recvs = [
        lax.ppermute(x, axes, plan.pairs(high_step=r + 1)) for r, x in enumerate(sends)
    ]
    factor = 1.0 / math.sqrt(nd * ng * ng * tile_h * tile_w)
    out_rows = -(-plan.shard // LANES)
    shard, grads = call(
        functools.partial(last_kernel, plan, factor),
        (own, held, *recvs),
        [
            jax.ShapeDtypeStruct((out_rows, LANES), F32),
            jax.ShapeDtypeStruct(tiles.shape, BF16),
        ],
        [pltpu.VMEM((plan.rows + 8, LANES), F32)],
        name="last",
    )
    shard = shard.reshape(1, -1)[:, : plan.shard]
    return (outputs[None, None], grads[None, None], shard)


def solution(mesh):
    tiled = P("dp", "group", None, None, None, None)
    return jax.shard_map(
        per_device,
        mesh=mesh,
        in_specs=(tiled, tiled, P("dp", "group")) + (P(),) * 10,
        out_specs=(tiled, tiled, P(("dp", "group"), None)),
        check_vma=False,
    )
```
